32 devices in a mesh: seq: 32 (over z, y, x, core), tensor: 1.
Axes of the slice: x: 2, y: 2, z: 4, core: 2. Of those that a mesh axis runs over, the one named last changes fastest.
Arguments:
- layer_input: bfloat16 [8192, 2048], P('seq', 'tensor'), may hold values from -1.5 to 1.5
- queries: bfloat16 [8192, 4096], P('seq', 'tensor'), may hold values from -160 to 160
- key_values: bfloat16 [2, 8192, 1024], P(None, 'seq', 'tensor'), may hold values from -4.5 to 4.5
- attention_out: bfloat16 [8192, 4096], P('seq', 'tensor'), may hold values from -6 to 6
- output_grad: bfloat16 [8192, 4096], P('seq', 'tensor'), may hold values from -24 to 24
- document_start: int32 [8192], P('seq'), may hold values from 0 to 8191, as said below
Outputs:
- query_grad: bfloat16 [8192, 4096], P('seq', 'tensor')
- key_value_grad: bfloat16 [2, 8192, 1024], P(None, 'seq', 'tensor')
- query_weight_grad: float32 [2048, 4096], P('seq', 'tensor')
The draws below stay inside these ranges and needn't reach their ends.
Inputs may be any that keep to these rules, and one draw needn't show every extreme that they name: Non-decreasing; entry i is the position of the first token of token i's document, so i - 512 < document_start[i] <= i and document_start[document_start[i]] = document_start[i]; some token lies exactly 511 positions after its document's first token.
All inputs are finite; a program needn't handle non-finite values.
Results may differ from the reference program's by a relative error of at most 0.008.
Values may be sent and summed in bfloat16 or wider, within the bound.
A program may use at most 192 MiB of HBM per device.

```python
import math
import jax
import jax.numpy as jnp
from jax import lax

HEADS = 32
KV_HEADS = 8
HD = 128
D_IN = 2048
TOK_DEV = 256
REACH = 2
MOST = 512
TOKENS = 8192


def document_layout(key):
    lengths = jax.random.randint(jax.random.fold_in(key, 11), (TOKENS,), MOST // 4, MOST + 1)
    chosen = jax.random.randint(jax.random.fold_in(key, 12), (), 0, 4)
    position = jnp.arange(TOKENS, dtype=jnp.int32)
    lengths = jnp.where(position == chosen, MOST, lengths).astype(jnp.int32)
    finish = jnp.cumsum(lengths)
    begins = finish - lengths
    marks = jnp.zeros((TOKENS,), jnp.int32).at[begins].set(1, mode='drop')
    return lax.cummax(jnp.where(marks > 0, position, 0), axis=0).astype(jnp.int32)


def attention_pair(key):
    key_rows = jnp.clip(jax.random.normal(jax.random.fold_in(key, 21), (TOKENS, KV_HEADS, HD), jnp.float32), -4.5, 4.5)
    value_rows = jnp.clip(jax.random.normal(jax.random.fold_in(key, 22), (TOKENS, KV_HEADS, HD), jnp.float32), -4.5, 4.5)
    query_rows = jnp.clip(jax.random.normal(jax.random.fold_in(key, 23), (TOKENS, HEADS, HD), jnp.float32), -4.5, 4.5)
    pairs = jnp.stack((key_rows.reshape(TOKENS, KV_HEADS * HD), value_rows.reshape(TOKENS, KV_HEADS * HD)))
    return (query_rows.reshape(TOKENS, HEADS * HD), pairs)


def draw_document_start(key, part):
    return document_layout(key)


def draw_queries(key, part):
    return attention_pair(key)[0].astype(jnp.bfloat16)


def draw_key_values(key, part):
    return attention_pair(key)[1].astype(jnp.bfloat16)


def with_spikes(result, key, source, target, parts, factor):
    def block_of(dim):
        return (jnp.arange(result.shape[dim]) // (result.shape[dim] // parts)).reshape((-1,) + (1,) * (result.ndim - 1 - dim))

    near = jax.random.permutation(key, parts)[block_of(target)]
    second = (block_of(target) + parts // 2) % parts
    return jnp.where((block_of(source) == near) | (block_of(source) == second), factor * result, result)


def levels(stream_key, dims, pieces, low, largest):
    def one(axis_at, blocks):
        draws = jax.random.uniform(jax.random.fold_in(jax.random.fold_in(stream_key, 6), axis_at), (blocks,), jnp.float32, low / len(pieces), largest / len(pieces))
        return jnp.repeat(jnp.exp(draws), dims[axis_at] // blocks).reshape((-1,) + (1,) * (len(dims) - axis_at - 1))

    level = one(*pieces[0])
    for cut in pieces[1:]:
        level = level * one(*cut)
    return level


def centred(stream_key, shape, scale, most, shards=(), kind=jnp.bfloat16):
    values = scale * jax.random.normal(stream_key, shape, jnp.float32)
    if shards:
        values = values * levels(stream_key, shape, shards, -0.22, 0.18)
    return jnp.clip(values, -most, most).astype(kind)


def noise_with(stream_key, extent, width, bound, pieces, heavy, kind=jnp.bfloat16):
    entries = width * jax.random.normal(stream_key, extent, jnp.float32)
    if pieces:
        entries = entries * levels(stream_key, extent, pieces, -0.22, 0.18)
    return jnp.clip(with_spikes(entries, jax.random.fold_in(stream_key, 3), *heavy), -bound, bound).astype(kind)


def setup_inputs(seed: int = 0) -> dict:
    seeds = jax.random.split(jax.random.key(seed), 7)
    return {
        "layer_input": noise_with(seeds[0], (TOKENS, D_IN), 0.25, 1.5, ((0, 32),), (0, 1, 32, 2.75)),
        "queries": draw_queries(jax.random.fold_in(seeds[6], 71), 0),
        "key_values": draw_key_values(jax.random.fold_in(seeds[6], 71), 0),
        "attention_out": centred(seeds[3], (TOKENS, HEADS * HD), 1.0, 6.0, ((0, 32),)),
        "output_grad": centred(seeds[4], (TOKENS, HEADS * HD), 4.0, 24.0, ((0, 32),)),
        "document_start": draw_document_start(jax.random.fold_in(seeds[6], 71), 0),
    }


def reference(layer_input, queries, key_values, attention_out, output_grad, document_start):
    repeat = HEADS // KV_HEADS
    scaling = 1.0 / math.sqrt(HD)
    margin = REACH * TOK_DEV
    window = margin + TOK_DEV
    padded_pairs = jnp.concatenate([jnp.zeros((2, margin, KV_HEADS * HD), key_values.dtype), key_values], axis=1)
    offsets = jnp.arange(TOK_DEV, dtype=jnp.int32)
    window_offsets = jnp.arange(window, dtype=jnp.int32)
    highest = lax.Precision.HIGHEST

    def one_block(carry_grads, index):
        first_row = (index * TOK_DEV).astype(jnp.int32)
        query_heads = lax.dynamic_slice_in_dim(queries, first_row, TOK_DEV, 0).astype(jnp.float32).reshape(TOK_DEV, KV_HEADS, repeat, HD)
        grad_heads = lax.dynamic_slice_in_dim(output_grad, first_row, TOK_DEV, 0).astype(jnp.float32).reshape(TOK_DEV, KV_HEADS, repeat, HD)
        output_heads = lax.dynamic_slice_in_dim(attention_out, first_row, TOK_DEV, 0).astype(jnp.float32).reshape(TOK_DEV, KV_HEADS, repeat, HD)
        starts = lax.dynamic_slice_in_dim(document_start, first_row, TOK_DEV, 0)
        pair_block = lax.dynamic_slice_in_dim(padded_pairs, first_row, window, 1).astype(jnp.float32)
        key_heads = pair_block[0].reshape(window, KV_HEADS, HD)
        value_heads = pair_block[1].reshape(window, KV_HEADS, HD)
        query_pos = first_row + offsets
        key_pos = first_row - margin + window_offsets
        allowed = (key_pos[None, :] >= starts[:, None]) & (key_pos[None, :] <= query_pos[:, None])
        scores = jnp.einsum('igrd,jgd->grij', query_heads, key_heads, precision=highest) * scaling
        scores = jnp.where(allowed[None, None], scores, -jnp.inf)
        row_max = lax.optimization_barrier(jnp.max(scores, axis=3))
        log_total = row_max + jnp.log(lax.optimization_barrier(jnp.sum(jnp.exp(scores - row_max[..., None]), axis=3)))
        weights = jnp.exp(scores - log_total[..., None])
        weights_half = lax.optimization_barrier(weights.astype(jnp.bfloat16)).astype(jnp.float32)
        row_delta = lax.optimization_barrier(jnp.sum(grad_heads * output_heads, axis=3)).transpose(1, 2, 0)
        value_part = jnp.einsum('grij,igrd->jgd', weights_half, grad_heads, precision=highest)
        dot_grad = jnp.einsum('igrd,jgd->grij', grad_heads, value_heads, precision=highest)
        score_grad = (weights * (dot_grad - row_delta[..., None]) * scaling).astype(jnp.bfloat16)
        score_grad = lax.optimization_barrier(score_grad).astype(jnp.float32)
        query_part = jnp.einsum('grij,jgd->igrd', score_grad, key_heads, precision=highest).reshape(TOK_DEV, HEADS * HD)
        key_part = jnp.einsum('grij,igrd->jgd', score_grad, query_heads, precision=highest)
        update = jnp.stack((key_part.reshape(window, KV_HEADS * HD), value_part.reshape(window, KV_HEADS * HD)))
        previous = lax.dynamic_slice_in_dim(carry_grads, first_row, window, 1)
        carry_grads = lax.dynamic_update_slice_in_dim(carry_grads, previous + update, first_row, 1)
        return (carry_grads, query_part)
    initial = jnp.zeros((2, margin + TOKENS, KV_HEADS * HD), jnp.float32)
    indices = jnp.arange(TOKENS // TOK_DEV, dtype=jnp.int32)
    summed, query_blocks = lax.scan(one_block, initial, indices)
    query_grad = query_blocks.reshape(TOKENS, HEADS * HD).astype(jnp.bfloat16)
    key_value_grad = summed[:, margin:, :].astype(jnp.bfloat16)
    query_weight_grad = jnp.dot(layer_input.T, query_grad, preferred_element_type=jnp.float32)
    return (query_grad, key_value_grad, query_weight_grad)
```

```python
import functools
import math

import jax
import jax.numpy as jnp
from jax import lax
from jax.experimental import pallas as pl
from jax.experimental.pallas import tpu as pltpu
from jax.sharding import PartitionSpec as P

HEADS = 32
KV_HEADS = 8
HD = 128
REACH = 2
NEG = -1e30


def passed_along(shard, axis, by):
    size = lax.axis_size(axis)
    pairs = [(i, i + by) for i in range(size) if 0 <= i + by < size]
    return lax.ppermute(shard, axis, pairs)


def to_partner(x):
    size = lax.axis_size("seq")
    return lax.ppermute(x, "seq", [(i, i ^ 1) for i in range(size)])


NT = (((1,), (1,)), ((), ()))
NN = (((1,), (0,)), ((), ()))


def attention_kernel(
    repeat, starts_ref, delta_ref, q_ref, g_ref, kv2_ref, kv1_ref, kv0_ref,
    dq_ref, part2_ref, part1_ref, part0_ref, bias_ref,
):
    tok = q_ref.shape[0]
    window = bias_ref.shape[0]
    scaling = 1.0 / math.sqrt(HD)
    factor = scaling * math.log2(math.e)

    @pl.when(pl.program_id(0) == 0)
    def _():
        key_pos = lax.broadcasted_iota(jnp.int32, (window, tok), 0) - (window - tok)
        query_pos = lax.broadcasted_iota(jnp.int32, (window, tok), 1)
        allowed = (key_pos >= starts_ref[...]) & (key_pos <= query_pos)
        bias_ref[...] = jnp.where(allowed, 0.0, NEG)

    keys = jnp.concatenate((kv2_ref[0], kv1_ref[0], kv0_ref[0]), axis=0)
    values = jnp.concatenate((kv2_ref[1], kv1_ref[1], kv0_ref[1]), axis=0)
    keys_t = keys.T
    key_part = jnp.zeros((window, HD), jnp.float32)
    value_part = jnp.zeros((window, HD), jnp.float32)
    for head in range(repeat):
        lanes = slice(head * HD, (head + 1) * HD)
        q = q_ref[:, lanes]
        g = g_ref[:, lanes]
        scores = lax.dot_general(keys, q, NT, preferred_element_type=jnp.float32)
        scores = scores * factor + bias_ref[...]
        top = jnp.max(scores, axis=0, keepdims=True)
        weights = jnp.exp2(scores - top)
        weights = weights * (1.0 / jnp.sum(weights, axis=0, keepdims=True))
        dots = lax.dot_general(values, g, NT, preferred_element_type=jnp.float32)
        score_grad = (
            weights * (dots - delta_ref[0, head : head + 1, :]) * scaling
        ).astype(jnp.bfloat16)
        value_part += lax.dot_general(
            weights.astype(jnp.bfloat16), g, NN, preferred_element_type=jnp.float32
        )
        key_part += lax.dot_general(score_grad, q, NN, preferred_element_type=jnp.float32)
        dq_t = lax.dot_general(keys_t, score_grad, NN, preferred_element_type=jnp.float32)
        dq_ref[:, lanes] = dq_t.T.astype(dq_ref.dtype)
    for step, ref in enumerate((part2_ref, part1_ref, part0_ref)):
        rows = slice(step * tok, (step + 1) * tok)
        ref[0] = key_part[rows].astype(ref.dtype)
        ref[1] = value_part[rows].astype(ref.dtype)


def attention(first, count, repeat, starts, delta, queries, output_grad, kv2, kv1, kv0):
    tok = queries.shape[0]
    window = (REACH + 1) * tok
    wide = repeat * HD
    heads_spec = pl.BlockSpec((tok, wide), lambda g: (0, first + g))
    pair_spec = pl.BlockSpec((2, tok, HD), lambda g: (0, 0, first + g))
    out_pair = pl.BlockSpec((2, tok, HD), lambda g: (0, 0, g))
    flops = 10 * count * repeat * tok * window * HD
    return pl.pallas_call(
        functools.partial(attention_kernel, repeat),
        grid=(count,),
        in_specs=[
            pl.BlockSpec((1, tok), lambda g: (0, 0)),
            pl.BlockSpec((1, repeat, tok), lambda g: (first + g, 0, 0)),
            heads_spec,
            heads_spec,
            pair_spec,
            pair_spec,
            pair_spec,
        ],
        out_specs=[pl.BlockSpec((tok, wide), lambda g: (0, g)), out_pair, out_pair, out_pair],
        out_shape=[
            jax.ShapeDtypeStruct((tok, count * wide), jnp.bfloat16),
            jax.ShapeDtypeStruct((2, tok, count * HD), jnp.bfloat16),
            jax.ShapeDtypeStruct((2, tok, count * HD), jnp.float32),
            jax.ShapeDtypeStruct((2, tok, count * HD), jnp.float32),
        ],
        scratch_shapes=[pltpu.VMEM((window, tok), jnp.float32)],
        compiler_params=pltpu.CompilerParams(
            dimension_semantics=("arbitrary",), vmem_limit_bytes=48 * 1024 * 1024
        ),
        cost_estimate=pl.CostEstimate(
            flops=2 * flops,
            bytes_accessed=count * tok * HD * (6 * repeat + 32),
            transcendentals=count * repeat * tok * window,
        ),
    )(starts, delta, queries, output_grad, kv2, kv1, kv0)


LEAD = (2, 0, 1)


def chunk_sizes(groups):
    most = -(-groups // len(LEAD))
    least = groups - (len(LEAD) - 1) * most
    return (least,) + (most,) * (len(LEAD) - 1) if least > 0 else (groups,)


def summed_rows(features, grads, rows, chips, lead):
    bits = [1 << k for k in range(chips.bit_length() - 1)]
    bits = [bits[lead]] + bits[:lead] + bits[lead + 1 :]
    places = [0]
    for bit in reversed(bits):
        places = places + [place + bit for place in places]
    features = jnp.concatenate([features[p * rows : (p + 1) * rows] for p in places], axis=0)
    half = features.shape[0] // 2
    outgoing, total = (
        lax.dot_general(part, grads, NN, preferred_element_type=jnp.float32)
        for part in (features[half:], features[:half])
    )
    outgoing = outgoing.astype(jnp.bfloat16)
    size = 2 * chips
    for stage, bit in enumerate(bits):
        if stage:
            half = total.shape[0] // 2
            outgoing, total = total[half:].astype(jnp.bfloat16), total[:half]
        arrived = lax.ppermute(outgoing, "seq", [(i, i ^ (2 * bit)) for i in range(size)])
        total = total + arrived.astype(jnp.float32)
    return total


def shards(layer_input, queries, key_values, attention_out, output_grad, document_start):
    tok_rows = queries.shape[0]
    groups = key_values.shape[2] // HD
    repeat = HEADS // KV_HEADS
    size = lax.axis_size("seq")
    shard_index = lax.axis_index("seq")
    core = shard_index % 2
    kv1 = passed_along(key_values, "seq", 1)
    kv2 = passed_along(kv1, "seq", 1)

    chip = shard_index // 2
    chips = size // 2
    features = lax.all_gather(layer_input, "tensor", axis=1, tiled=True).T
    own_rows = features.shape[0] // size
    kept, given = (
        jnp.concatenate(
            [
                lax.dynamic_slice_in_dim(
                    features, (2 * (chip ^ place) + side) * own_rows, own_rows, 0
                )
                for place in range(chips)
            ],
            axis=0,
        )
        for side in (core, 1 - core)
    )
    features = jnp.concatenate((kept, to_partner(given)), axis=1)

    starts = (document_start - shard_index * tok_rows).reshape(1, tok_rows)
    delta = jnp.sum(
        output_grad.astype(jnp.float32).reshape(tok_rows, groups * repeat, HD)
        * attention_out.astype(jnp.float32).reshape(tok_rows, groups * repeat, HD),
        axis=2,
    ).T.reshape(groups, repeat, tok_rows)

    query_parts, pair_parts, weight_parts = [], [], []
    first = 0
    for chunk, count in enumerate(chunk_sizes(groups)):
        dq, part2, part1, part0 = attention(
            first, count, repeat, starts, delta, queries, output_grad, kv2, kv1, key_values
        )
        first += count
        both = jnp.concatenate((dq, to_partner(dq)), axis=0)
        weight_parts.append(summed_rows(features, both, own_rows, chips, LEAD[chunk]))
        pair = (passed_along(part2, "seq", -1).astype(jnp.float32) + part1).astype(jnp.bfloat16)
        pair = (passed_along(pair, "seq", -1).astype(jnp.float32) + part0).astype(jnp.bfloat16)
        query_parts.append(dq)
        pair_parts.append(pair)
    return (
        jnp.concatenate(query_parts, axis=1),
        jnp.concatenate(pair_parts, axis=2),
        jnp.concatenate(weight_parts, axis=1),
    )


def solution(mesh):
    placed = (
        P("seq", "tensor"),
        P("seq", "tensor"),
        P(None, "seq", "tensor"),
        P("seq", "tensor"),
        P("seq", "tensor"),
        P("seq"),
    )
    return jax.shard_map(
        shards,
        mesh=mesh,
        in_specs=placed,
        out_specs=(P("seq", "tensor"), P(None, "seq", "tensor"), P("seq", "tensor")),
        check_vma=False,
    )
```
